32 devices in a mesh: ctx: 8 (over z, y), head: 4 (over x, core).
Axes of the slice: x: 2, y: 2, z: 4, core: 2. Of those that a mesh axis runs over, the one named last changes fastest.
Arguments:
- mixer_input: bfloat16 [4096, 8192], P(('ctx', 'head')), may hold values from -0.0625 to 0.0625
- write_vectors: bfloat16 [4096, 1024], P(('ctx', 'head')), may hold values from -0.1875 to 0.1875
- read_vectors: bfloat16 [4096, 1024], P(('ctx', 'head')), may hold values from -0.1875 to 0.1875
- step_sizes: bfloat16 [4096, 128], P(('ctx', 'head')), may hold values from 0.5 to 2867
- fast_rates: float32 [128], replicated, may hold values from 1.2207031e-05 to 0.034
- slow_heads: int32 [64], replicated, may hold values from 0 to 127, as said below
- skip_gains: float32 [128], replicated, may hold values from 0.5 to 1.5
- mixer_grad: bfloat16 [4096, 8192], P(('ctx', 'head')), may hold values from -6 to 6
- queries: bfloat16 [4096, 4096], P(('ctx', 'head')), may hold values from -150 to 150
- attn_keys: bfloat16 [4096, 1024], P(('ctx', 'head')), may hold values from -6 to 6
- attn_values: bfloat16 [4096, 1024], P(('ctx', 'head')), may hold values from -24 to 24
- attn_grad: bfloat16 [4096, 4096], P(('ctx', 'head')), may hold values from -24 to 24
- doc_lengths: int32 [16], replicated, may hold values from 1 to 1536, 4096 in all
Outputs:
- grad_mixer_input: bfloat16 [4096, 8192], P(('ctx', 'head'))
- grad_write: bfloat16 [4096, 1024], P(('ctx', 'head'))
- grad_read: bfloat16 [4096, 1024], P(('ctx', 'head'))
- grad_queries: bfloat16 [4096, 4096], P(('ctx', 'head'))
The draws below stay inside these ranges and needn't reach their ends.
Inputs may be any that keep to these rules, and one draw needn't show every extreme that they name: `slow_heads`: distinct head numbers.
All inputs are finite; a program needn't handle non-finite values.
Results may differ from the reference program's by a relative error of at most 0.0062.
Values may be sent and summed in bfloat16 or wider, within the bound.
No kernel may reach another device: no remote copies, remote signals or barrier semaphores. Data moves between devices by JAX's collectives and lax.ppermute only.
A program may use at most 192 MiB of HBM per device.

```python
import math
import jax
import jax.numpy as jnp
import numpy as np
from jax import lax

MH = 128
HD = 64
GROUPS = 8
NS = 128
QH = 32
KVH = 8
DH = 128
BLOCK = 256
DOCS = 16
SLOW = 64
SLAB_TOKENS = 4096
DOC_MOST = 1536


def paired_attention(key):
    base_offset = jax.random.fold_in(key, 7)
    keys_drawn = jnp.clip(jax.random.normal(jax.random.fold_in(base_offset, 1), (SLAB_TOKENS, KVH * DH), jnp.float32), -6.0, 6.0)
    queries_drawn = jnp.clip(jax.random.normal(jax.random.fold_in(base_offset, 2), (SLAB_TOKENS, QH * DH), jnp.float32), -6.0, 6.0)
    return (queries_drawn, keys_drawn)


def draw_queries(key, part):
    return paired_attention(key)[0].astype(jnp.bfloat16)


def draw_attn_keys(key, part):
    return paired_attention(key)[1].astype(jnp.bfloat16)


def draw_step_sizes(key, part):
    base_offset = jax.random.fold_in(key, 21)
    sampled_steps = jnp.exp(jax.random.uniform(jax.random.fold_in(base_offset, 1), (SLAB_TOKENS, MH), jnp.float32, math.log(0.5), math.log(2.0)))
    flurry_rows = jax.random.randint(jax.random.fold_in(base_offset, 2), (4,), 0, SLAB_TOKENS)
    flurry_lengths = jax.random.uniform(jax.random.fold_in(base_offset, 3), (4, 1), jnp.float32, 0.22, 0.69) * SLAB_TOKENS
    match_count = jnp.arange(SLAB_TOKENS)[None, :] == flurry_rows[:, None]
    flurry_groups = jnp.max(jnp.where(match_count, flurry_lengths, 0.0), axis=0)
    return jnp.maximum(sampled_steps, flurry_groups[:, None]).astype(jnp.bfloat16)


def draw_fast_rates(key, part):
    base_offset = jax.random.fold_in(key, 31)
    drawn = jnp.exp(jax.random.uniform(base_offset, (MH,), jnp.float32, math.log(1.0 / 50.0), math.log(1.0 / 30.0)))
    return drawn


def draw_slow_heads(key, part):
    return jax.random.permutation(jax.random.fold_in(key, 41), MH)[:SLOW].astype(jnp.int32)


def steps_of(stream_key, extent, split, least, high):
    def one(axis_at, parts):
        steps = jax.random.uniform(jax.random.fold_in(jax.random.fold_in(stream_key, 6), axis_at), (parts,), jnp.float32, least / len(split), high / len(split))
        return jnp.repeat(jnp.exp(steps), extent[axis_at] // parts).reshape((-1,) + (1,) * (len(extent) - axis_at - 1))

    gain = one(*split[0])
    for cut in split[1:]:
        gain = gain * one(*cut)
    return gain


def split_up(count, total, reach, skew):
    loads = [(1 << 20) // math.isqrt(rank ** skew) + 1 for rank in range(2, count + 1)]
    spare, counts = total - reach - (count - 1), [1] * (count - 1)
    while spare > 0:
        candidates = [i for i in range(count - 1) if counts[i] < reach]
        whole, remaining = sum([loads[i] for i in candidates]), spare
        for i in candidates:
            extra = min(reach - counts[i], max(1, remaining * loads[i] // whole), spare)
            counts[i] = counts[i] + extra
            spare = spare - extra
    return np.array([reach] + counts)


def uneven_parts(stream_key, amount, total, limit, skew):
    if amount == 2:
        one = jax.random.randint(stream_key, (), max(1, total - limit), min(limit, total - 1) + 1)
        return jnp.stack([one, total - one])
    sizes = jnp.asarray(split_up(amount, total, limit, skew), jnp.int32)
    twos = (amount - 1) // 2
    donor, sink = sizes[1:1 + 2 * twos:2], sizes[2:2 + 2 * twos:2]
    room = jnp.minimum(donor - 1, limit - sink)
    moved = jax.random.randint(jax.random.fold_in(stream_key, 1), (twos,), 0, 1 << 20) % (room + 1)
    sizes = sizes.at[1:1 + 2 * twos:2].set(donor - moved).at[2:2 + 2 * twos:2].set(sink + moved)
    return sizes[jax.random.permutation(jax.random.fold_in(stream_key, 2), amount)]


def normal_values(own_key, extent, width, bound, pieces=(), held_as=jnp.bfloat16):
    result = width * jax.random.normal(own_key, extent, jnp.float32)
    if pieces:
        result = result * steps_of(own_key, extent, pieces, -0.22, 0.18)
    return jnp.clip(result, -bound, bound).astype(held_as)


def setup_inputs(seed: int = 0) -> dict:
    key_of = jax.random.split(jax.random.key(seed), 14)
    return {
        "mixer_input": normal_values(key_of[0], (SLAB_TOKENS, MH * HD), 0.01, 0.0625, ((0, 32),)),
        "write_vectors": normal_values(key_of[1], (SLAB_TOKENS, GROUPS * NS), 0.03, 0.1875, ((0, 32),)),
        "read_vectors": normal_values(key_of[2], (SLAB_TOKENS, GROUPS * NS), 0.03, 0.1875, ((0, 32),)),
        "step_sizes": draw_step_sizes(jax.random.fold_in(key_of[13], 71), 0),
        "fast_rates": draw_fast_rates(jax.random.fold_in(key_of[13], 71), 0),
        "slow_heads": draw_slow_heads(jax.random.fold_in(key_of[13], 71), 0),
        "skip_gains": jnp.clip(jax.random.uniform(key_of[6], (MH,), jnp.float32, 0.5, 1.5), 0.5, 1.5),
        "mixer_grad": normal_values(key_of[7], (SLAB_TOKENS, MH * HD), 1.0, 6.0, ((0, 32),)),
        "queries": draw_queries(jax.random.fold_in(key_of[13], 71), 0),
        "attn_keys": draw_attn_keys(jax.random.fold_in(key_of[13], 71), 0),
        "attn_values": normal_values(key_of[10], (SLAB_TOKENS, KVH * DH), 4.0, 24.0, ((0, 32),)),
        "attn_grad": normal_values(key_of[11], (SLAB_TOKENS, QH * DH), 4.0, 24.0, ((0, 32),)),
        "doc_lengths": uneven_parts(key_of[12], DOCS, SLAB_TOKENS, DOC_MOST, 2).astype(jnp.int32),
    }


HIGH = lax.Precision.HIGHEST


def rounded(values):
    return lax.optimization_barrier(values.astype(jnp.bfloat16)).astype(jnp.float32)


def doc_index(positions, doc_lengths):
    starts = (jnp.cumsum(doc_lengths) - doc_lengths).astype(jnp.int32)
    match_count = (starts[None, :] <= positions[:, None]).astype(jnp.int32)
    return (jnp.sum(match_count, axis=1) - 1).astype(jnp.int32)


def stretch_edges_ref(stretch_inputs, stretch_write, stretch_read, decay_log, stretch_grads, docs, doc_prev):
    cumulative = jnp.cumsum(decay_log, axis=1)
    totals = cumulative[:, -1]
    linked = (docs == doc_prev[:, None]).astype(jnp.float32)
    tail_doc = (docs == docs[:, -1:]).astype(jnp.float32)
    stretch_links = jnp.exp(totals) * linked[:, -1][:, None, None]
    entering = jnp.exp(cumulative) * linked[:, :, None, None]
    to_end = jnp.exp(totals[:, None] - cumulative) * tail_doc[:, :, None, None]
    input_weighted = rounded(stretch_inputs * to_end[..., None])
    grad_weighted = rounded(stretch_grads * entering[..., None])
    endings = jnp.einsum("ksghp,ksgn->kghpn", input_weighted, stretch_write, precision=HIGH)
    openings = jnp.einsum("ktghp,ktgn->kghpn", grad_weighted, stretch_read, precision=HIGH)
    return cumulative, stretch_links, to_end, input_weighted, grad_weighted, endings, openings


def stretch_inner_ref(stretch_inputs, stretch_write, stretch_read, stretch_grads, docs, cumulative):
    block_rows = stretch_inputs.shape[1]
    offsets = jnp.arange(block_rows, dtype=jnp.int32)
    causal = offsets[:, None] >= offsets[None, :]
    same_doc = causal[None] & (docs[:, :, None] == docs[:, None, :])
    cum_heads = jnp.transpose(cumulative, (0, 2, 3, 1))
    log_gaps = cum_heads[..., :, None] - cum_heads[..., None, :]
    decays = jnp.exp(jnp.where(same_doc[:, None, None], log_gaps, -jnp.inf))
    scores = jnp.einsum("ktgn,ksgn->kgts", stretch_read, stretch_write, precision=HIGH)
    mixing = rounded(scores[:, :, None] * decays)
    input_inner = jnp.einsum("kghts,ktghp->ksghp", mixing, stretch_grads, precision=HIGH)
    inner_products = jnp.einsum("ktghp,ksghp->kghts", stretch_grads, stretch_inputs, precision=HIGH)
    joint_weights = rounded(jnp.sum(inner_products * decays, axis=2))
    read_inner = jnp.einsum("kgts,ksgn->ktgn", joint_weights, stretch_write, precision=HIGH)
    write_inner = jnp.einsum("kgts,ktgn->ksgn", joint_weights, stretch_read, precision=HIGH)
    return input_inner, write_inner, read_inner


def mixer_reference(mixer_input, write_vectors, read_vectors, step_sizes, fast_rates, slow_heads, skip_gains, mixer_grad, doc_lengths):
    per_group = MH // GROUPS
    stretch_count = SLAB_TOKENS // BLOCK
    head_ids = jnp.arange(MH, dtype=jnp.int32)
    slow_mask = jnp.any(head_ids[:, None] == slow_heads[None, :], axis=1)
    rates = jnp.where(slow_mask, 1.0 / SLAB_TOKENS, fast_rates).reshape(GROUPS, per_group)
    skip_here = skip_gains.reshape(GROUPS, per_group)
    shape_x = (stretch_count, 1, BLOCK, GROUPS, per_group, HD)
    shape_v = (stretch_count, 1, BLOCK, GROUPS, NS)
    positions = jnp.arange(SLAB_TOKENS, dtype=jnp.int32)
    docs = doc_index(positions, doc_lengths).reshape(stretch_count, 1, BLOCK)
    doc_prev = doc_index(positions[::BLOCK] - 1, doc_lengths).reshape(stretch_count, 1)
    decay_log = -step_sizes.astype(jnp.float32).reshape(stretch_count, 1, BLOCK, GROUPS, per_group) * rates
    items = (mixer_input.reshape(shape_x), write_vectors.reshape(shape_v), read_vectors.reshape(shape_v), decay_log, mixer_grad.reshape(shape_x), docs, doc_prev)

    def widen(element):
        return (element[0].astype(jnp.float32), element[1].astype(jnp.float32), element[2].astype(jnp.float32), element[3], element[4].astype(jnp.float32), element[5], element[6])

    def backward_step(carried, element):
        stretch_parts = stretch_edges_ref(*widen(element))
        return stretch_parts[6][0] + stretch_parts[1][0][..., None, None] * carried, carried

    zero_state = jnp.zeros((GROUPS, per_group, HD, NS), jnp.float32)
    unused, back_states = lax.scan(backward_step, zero_state, items, reverse=True)

    def forward_step(carried, element):
        stretch_inputs, stretch_write, stretch_read, stretch_decay, stretch_grads, stretch_docs, stretch_prev = widen(element[:7])
        back_state = rounded(element[7])
        state_low = rounded(carried)
        cumulative, stretch_links, to_end, input_weighted, grad_weighted, endings, openings = stretch_edges_ref(stretch_inputs, stretch_write, stretch_read, stretch_decay, stretch_grads, stretch_docs, stretch_prev)
        input_inner, write_inner, read_inner = stretch_inner_ref(stretch_inputs, stretch_write, stretch_read, stretch_grads, stretch_docs, cumulative)
        read_carried = jnp.einsum("ktghp,kghpn->ktgn", grad_weighted, state_low[None], precision=HIGH)
        write_carried = jnp.einsum("ksghp,kghpn->ksgn", input_weighted, back_state[None], precision=HIGH)
        input_carried = to_end[..., None] * jnp.einsum("ksgn,kghpn->ksghp", stretch_write, back_state[None], precision=HIGH)
        grad_input = (input_inner + input_carried + skip_here[..., None] * stretch_grads).astype(jnp.bfloat16)
        grad_write = (write_inner + write_carried).astype(jnp.bfloat16)
        grad_read = (read_inner + read_carried).astype(jnp.bfloat16)
        following = stretch_links[0][..., None, None] * carried + endings[0]
        return following, (grad_input, grad_write, grad_read)

    unused, outputs = lax.scan(forward_step, zero_state, items + (back_states,))
    return (outputs[0].reshape(SLAB_TOKENS, MH * HD), outputs[1].reshape(SLAB_TOKENS, GROUPS * NS), outputs[2].reshape(SLAB_TOKENS, GROUPS * NS))


def attend_ref(query_block, grad_block, key_block, value_block, query_pos, key_pos, query_doc, key_doc):
    scaling = DH ** -0.5
    logits = jnp.einsum("qgrd,kgd->grqk", query_block.astype(jnp.float32), key_block.astype(jnp.float32), precision=HIGH) * scaling
    allowed = (key_pos[None, :] <= query_pos[:, None]) & (key_pos[None, :] >= 0) & (query_doc[:, None] == key_doc[None, :])
    logits = jnp.where(allowed, logits, -jnp.inf)
    row_peaks = jnp.max(logits, axis=-1, keepdims=True)
    weights = jnp.exp(logits - row_peaks)
    probabilities = weights / jnp.sum(weights, axis=-1, keepdims=True)
    grad_probs = jnp.einsum("qgrd,kgd->grqk", grad_block.astype(jnp.float32), value_block.astype(jnp.float32), precision=HIGH)
    centre = jnp.sum(probabilities * grad_probs, axis=-1, keepdims=True)
    grad_logits = rounded(probabilities * (grad_probs - centre))
    return jnp.einsum("grqk,kgd->qgrd", grad_logits, key_block.astype(jnp.float32), precision=HIGH) * scaling


def attention_reference(queries, attn_keys, attn_values, attn_grad, doc_lengths):
    group_size = QH // KVH
    block_rows = min(128, SLAB_TOKENS)
    query_four = queries.reshape(SLAB_TOKENS, KVH, group_size, DH)
    grad_four = attn_grad.reshape(SLAB_TOKENS, KVH, group_size, DH)
    padding = jnp.zeros((DOC_MOST, KVH * DH), jnp.bfloat16)
    key_three = jnp.concatenate([padding, attn_keys], axis=0).reshape(DOC_MOST + SLAB_TOKENS, KVH, DH)
    value_three = jnp.concatenate([padding, attn_values], axis=0).reshape(DOC_MOST + SLAB_TOKENS, KVH, DH)
    query_positions = jnp.arange(SLAB_TOKENS, dtype=jnp.int32)
    key_positions = jnp.arange(SLAB_TOKENS + DOC_MOST, dtype=jnp.int32) - DOC_MOST
    query_docs = doc_index(query_positions, doc_lengths)
    key_docs = doc_index(key_positions, doc_lengths)

    def one_block(index):
        begin = (index * block_rows).astype(jnp.int32)
        span = DOC_MOST + block_rows
        return attend_ref(
            lax.dynamic_slice_in_dim(query_four, begin, block_rows, 0),
            lax.dynamic_slice_in_dim(grad_four, begin, block_rows, 0),
            lax.dynamic_slice_in_dim(key_three, begin, span, 0),
            lax.dynamic_slice_in_dim(value_three, begin, span, 0),
            lax.dynamic_slice_in_dim(query_positions, begin, block_rows, 0),
            lax.dynamic_slice_in_dim(key_positions, begin, span, 0),
            lax.dynamic_slice_in_dim(query_docs, begin, block_rows, 0),
            lax.dynamic_slice_in_dim(key_docs, begin, span, 0))

    blocks = lax.map(one_block, jnp.arange(SLAB_TOKENS // block_rows, dtype=jnp.int32))
    return blocks.reshape(SLAB_TOKENS, QH * DH).astype(jnp.bfloat16)


def reference(mixer_input, write_vectors, read_vectors, step_sizes, fast_rates, slow_heads, skip_gains, mixer_grad, queries, attn_keys, attn_values, attn_grad, doc_lengths):
    grad_input, grad_write, grad_read = mixer_reference(mixer_input, write_vectors, read_vectors, step_sizes, fast_rates, slow_heads, skip_gains, mixer_grad, doc_lengths)
    grad_queries = attention_reference(queries, attn_keys, attn_values, attn_grad, doc_lengths)
    return (grad_input, grad_write, grad_read, grad_queries)
```

```python
import functools

import jax
import jax.numpy as jnp
from jax import lax
from jax.experimental import pallas as pl
from jax.experimental.pallas import tpu as pltpu
from jax.sharding import PartitionSpec as P

NS = 128
HD = 64
DH = 128
KEYS = 256
REACH = 3
AXES = ("ctx", "head")
F32 = jnp.float32
BF16 = jnp.bfloat16
NT = (((1,), (1,)), ((), ()))
TN = (((0,), (0,)), ((), ()))
STEPS = 32000.0
LINK = 2 * NS + 2


def dot(a, b, dims=None):
    if dims is None:
        return jnp.dot(a, b, preferred_element_type=F32)
    return lax.dot_general(a, b, dims, preferred_element_type=F32)


def split(a):
    high = a.astype(BF16)
    return high, (a - high.astype(F32)).astype(BF16)


def split3(a):
    high = a.astype(BF16).astype(F32)
    low = (a - high).astype(BF16).astype(F32)
    return high, low, a - high - low


def count_before(lengths, position):
    start = jnp.int32(0)
    count = jnp.zeros_like(position)
    for j in range(lengths.shape[0]):
        count += jnp.where(start <= position, 1, 0)
        start += lengths[j]
    return count


def doc_start(lengths, position):
    start = jnp.int32(0)
    begin = jnp.zeros_like(position)
    for j in range(lengths.shape[0]):
        begin = jnp.where(start <= position, start, begin)
        start += lengths[j]
    return begin


def head_rates(slow, fast, total_rows):
    ids = lax.broadcasted_iota(jnp.int32, fast.shape, 1)
    mask = ids < 0
    for j in range(slow.shape[0]):
        mask = mask | (ids == slow[j])
    return jnp.where(mask, F32(1.0 / total_rows), fast)


def running_sums(steps, rates):
    rows = steps.shape[0]
    later = lax.broadcasted_iota(jnp.int32, (rows, rows), 0)
    earlier = lax.broadcasted_iota(jnp.int32, (rows, rows), 1)
    lower = jnp.where(later >= earlier, 1.0, 0.0).astype(BF16)
    return -dot(lower, steps) * rates


def spread(group, heads, per_group):
    row = lax.broadcasted_iota(jnp.int32, (heads, per_group * HD), 0)
    column = lax.broadcasted_iota(jnp.int32, (heads, per_group * HD), 1)
    return jnp.where(row == group * per_group + column // HD, 1.0, 0.0).astype(BF16)


def edge_factors(place, lengths, cumulative):
    rows = cumulative.shape[0]
    base = place * rows
    total = cumulative[rows - 1 : rows, :]
    docs = count_before(lengths, base + lax.broadcasted_iota(jnp.int32, cumulative.shape, 0))
    last = count_before(lengths, base + rows - 1)
    before = count_before(lengths, base - 1)
    to_end = jnp.where(docs == last, jnp.exp(total - cumulative), 0.0)
    entering = jnp.where(docs == before, jnp.exp(cumulative), 0.0)
    link = jnp.where(last == before, jnp.exp(total), 0.0)
    return to_end, entering, link


def encode(value):
    top = jnp.max(jnp.abs(value), axis=0, keepdims=True)
    power = jnp.ceil(jnp.log(jnp.maximum(top, 1e-30)) * 1.4426950408889634)
    codes = jnp.round(value * (jnp.exp2(-power) * STEPS)).astype(jnp.int32)
    return codes.astype(jnp.int16), power


def unit_of(ref, row):
    return jnp.exp2(ref[row : row + 1, :].astype(F32)) * (1.0 / STEPS)


def link_of(ref, row):
    high, low = ref[row : row + 1, :].astype(F32), ref[row + 1 : row + 2, :].astype(F32)
    return (high + low * (1.0 / 32768)) * (1.0 / 16384)


def side_rows(*values):
    rows = lax.broadcasted_iota(jnp.int32, (16, values[0].shape[1]), 0)
    out = jnp.zeros(rows.shape, F32)
    for i, value in enumerate(values):
        out = jnp.where(rows == i, value, out)
    return out.astype(jnp.int32).astype(jnp.int16)


def link_codes(link):
    high = jnp.round(link * 16384)
    return high, jnp.round((link * 16384 - high) * 32768)


def following(kernel, inputs, extra):
    def body(*refs):
        return kernel(*refs[:inputs], *refs[inputs + extra :])

    return body


def edges_kernel(
    total_rows, per_group, info, lengths, slow, x, g, w, r, steps, fast, out, factors, links
):
    step = pl.program_id(0)
    heads = steps.shape[1]

    @pl.when(step == 0)
    def _():
        rates = head_rates(slow, fast[...], total_rows)
        cumulative = running_sums(steps[...], rates)
        to_end, entering, link = edge_factors(info[0], lengths, cumulative)
        factors[0], factors[1] = split(to_end)
        factors[2], factors[3] = split(entering)
        high, low, lowest = split3(link)
        row = lax.broadcasted_iota(jnp.int32, (16, heads), 0)
        table = jnp.where(row == 0, high, jnp.where(row == 1, low, jnp.where(row == 2, lowest, 0.0)))
        links[...] = table.astype(BF16)

    group = info[1] * pl.num_programs(0) + (info[2] ^ step)
    one_hot = spread(group, heads, per_group)
    to_end = dot(factors[0], one_hot) + dot(factors[1], one_hot)
    weighted = (x[...].astype(F32) * to_end).astype(BF16)
    out[0, 0:NS, :], power_e = encode(dot(w[...], weighted, TN))
    entering = dot(factors[2], one_hot) + dot(factors[3], one_hot)
    weighted = (g[...].astype(F32) * entering).astype(BF16)
    out[0, NS : 2 * NS, :], power_o = encode(dot(r[...], weighted, TN))
    link = jnp.sum(dot(links[...], one_hot), axis=0, keepdims=True)
    out[0, 2 * NS : 2 * NS + 16, :] = side_rows(power_e, power_o, *link_codes(link))


def edges(info, lengths, slow, x, g, w, r, steps, fast, total_rows):
    rows, heads = steps.shape
    groups = w.shape[1] // NS
    per_group = heads // groups
    width = per_group * HD
    half = groups // 2

    def column(i, info, lengths, slow):
        return (0, info[1] * half + (info[2] ^ i))

    return pl.pallas_call(
        functools.partial(edges_kernel, total_rows, per_group),
        out_shape=jax.ShapeDtypeStruct((half, 2 * NS + 16, width), jnp.int16),
        grid_spec=pltpu.PrefetchScalarGridSpec(
            num_scalar_prefetch=3,
            grid=(half,),
            in_specs=[
                pl.BlockSpec((rows, width), column),
                pl.BlockSpec((rows, width), column),
                pl.BlockSpec((rows, NS), column),
                pl.BlockSpec((rows, NS), column),
                pl.BlockSpec((rows, heads), lambda i, *_: (0, 0)),
                pl.BlockSpec((1, heads), lambda i, *_: (0, 0)),
            ],
            out_specs=pl.BlockSpec((1, 2 * NS + 16, width), lambda i, *_: (i, 0, 0)),
            scratch_shapes=[
                pltpu.VMEM((4, rows, heads), BF16),
                pltpu.VMEM((16, heads), BF16),
            ],
        ),
        cost_estimate=pl.CostEstimate(
            flops=rows * NS * width * half * 12, bytes_accessed=9 << 19, transcendentals=0
        ),
        name="edges",
    )(info, lengths, slow, x, g, w, r, steps, fast)


def pair_kernel(info, mine, other, *outs):
    first = info[2] == 0
    for r, out in enumerate(outs):
        link_mine, link_other = link_of(mine.at[r], LINK), link_of(other.at[r], LINK)
        one = jnp.ones_like(link_mine)
        powers = []
        for n, (a, b) in enumerate(
            (
                (jnp.where(first, link_other, one), jnp.where(first, one, link_mine)),
                (jnp.where(first, one, link_other), jnp.where(first, link_mine, one)),
            )
        ):
            cut = slice(n * NS, (n + 1) * NS)
            a = a * unit_of(mine.at[r], 2 * NS + n)
            b = b * unit_of(other.at[r], 2 * NS + n)
            out[cut, :], power = encode(
                mine[r, cut, :].astype(F32) * a + other[r, cut, :].astype(F32) * b
            )
            powers.append(power)
        out[2 * NS : 2 * NS + 16, :] = side_rows(*powers, *link_codes(link_mine * link_other))


VMEM = pl.BlockSpec(memory_space=pltpu.VMEM)
SMEM = pl.BlockSpec(memory_space=pltpu.SMEM)
ANY = pl.BlockSpec(memory_space=pl.ANY)


def pair(info, mine, other):
    half, rows, width = mine.shape
    return pl.pallas_call(
        pair_kernel,
        out_shape=[jax.ShapeDtypeStruct((rows, width), jnp.int16)] * half,
        in_specs=[SMEM, VMEM, VMEM],
        out_specs=[VMEM] * half,
        cost_estimate=pl.CostEstimate(flops=half * rows * width * 8, bytes_accessed=6 << 20, transcendentals=0),
        name="pair",
    )(info, mine, other)


def totals_kernel(count, info, *refs):
    ins, (forward, backward) = refs[:count], refs[count:]
    chip = info[1]
    links = [link_of(ref, LINK) for ref in ins]
    one = jnp.ones_like(links[0])
    sums = [None, None]
    product = one
    for r in range(count):
        after, before = one, one
        for s in range(count):
            if s != r:
                later = (chip ^ s) > (chip ^ r)
                after = after * jnp.where(later, links[s], one)
                before = before * jnp.where(later, one, links[s])
        for n, factor in enumerate((after, before)):
            part = ins[r][n * NS : (n + 1) * NS, :].astype(F32) * (factor * unit_of(ins[r], 2 * NS + n))
            sums[n] = part if r == 0 else sums[n] + part
        product = product * links[r]
    codes = link_codes(product)
    for total, out in zip(sums, (forward, backward)):
        out[0:NS, :], power = encode(total)
        out[NS : NS + 16, :] = side_rows(power, *codes)


def totals(info, parts, after):
    width = parts[0].shape[1]
    return pl.pallas_call(
        following(functools.partial(totals_kernel, len(parts)), 1 + len(parts), len(after)),
        out_shape=[jax.ShapeDtypeStruct((NS + 16, width), jnp.int16)] * 2,
        in_specs=[SMEM] + [VMEM] * len(parts) + [ANY] * len(after),
        out_specs=[VMEM] * 2,
        cost_estimate=pl.CostEstimate(flops=16 * NS * width, bytes_accessed=3 << 20, transcendentals=0),
        name="totals",
    )(info, *parts, *after)


def carry_kernel(count, shifts, info, *refs):
    ins = refs[:count]
    behind = refs[count : count + shifts]
    ahead = refs[count + shifts : count + 2 * shifts]
    outs = refs[count + 2 * shifts : 2 * count + 2 * shifts]
    ordered, result = refs[2 * count + 2 * shifts :]
    chip = info[1]
    for r in range(count):
        ordered[chip ^ r] = ins[r][...]
    links = [link_of(ordered.at[j], LINK) for j in range(count)]
    powers = [[None, None] for _ in range(count)]
    for n, (sources, order) in enumerate(
        ((behind, list(range(count))), (ahead, list(range(count - 1, -1, -1))))
    ):
        cut = slice(n * NS, (n + 1) * NS)
        state = sources[0][0:NS, :].astype(F32) * unit_of(sources[0], NS)
        factor = link_of(sources[0], NS + 1)
        for k in range(1, shifts):
            state = state + sources[k][0:NS, :].astype(F32) * (factor * unit_of(sources[k], NS))
            factor = factor * link_of(sources[k], NS + 1)
        for m, j in enumerate(order):
            result[j, cut, :], powers[j][n] = encode(state)
            if m < count - 1:
                state = (
                    ordered[j, cut, :].astype(F32) * unit_of(ordered.at[j], 2 * NS + n)
                    + links[j] * state
                )
    for j in range(count):
        result[j, 2 * NS : 2 * NS + 16, :] = side_rows(*powers[j])
    for r in range(count):
        outs[r][...] = result[chip ^ r]


def carry(info, parts, behind, ahead):
    rows, width = parts[0].shape
    count, shifts = len(parts), len(behind)
    return pl.pallas_call(
        functools.partial(carry_kernel, count, shifts),
        out_shape=[jax.ShapeDtypeStruct((rows, width), jnp.int16)] * count,
        in_specs=[SMEM] + [VMEM] * (count + 2 * shifts),
        out_specs=[VMEM] * count,
        scratch_shapes=[
            pltpu.VMEM((count, rows, width), jnp.int16),
            pltpu.VMEM((count, rows, width), jnp.int16),
        ],
        cost_estimate=pl.CostEstimate(flops=24 * NS * width, bytes_accessed=5 << 20, transcendentals=0),
        name="carry",
    )(info, *parts, *behind, *ahead)


def unpair_kernel(count, info, mine, other, *refs):
    ins, (kept, sent) = refs[:count], refs[count:]
    top, bottom = slice(0, NS), slice(NS, 2 * NS)
    for r in range(count):

        def entering(r):
            return (
                ins[r][top, :].astype(F32) * unit_of(ins[r], 2 * NS),
                ins[r][bottom, :].astype(F32) * unit_of(ins[r], 2 * NS + 1),
            )

        def moved(ref, n, value, r):
            part = ref[r, n * NS : (n + 1) * NS, :].astype(F32) * unit_of(ref.at[r], 2 * NS + n)
            return (part + link_of(ref.at[r], LINK) * value).astype(BF16)

        @pl.when(info[2] == 0)
        def _(r=r):
            state, back = entering(r)
            kept[r, top, :] = state.astype(BF16)
            sent[r, top, :] = moved(mine, 0, state, r)
            kept[r, bottom, :] = moved(other, 1, back, r)
            sent[r, bottom, :] = back.astype(BF16)

        @pl.when(info[2] == 1)
        def _(r=r):
            state, back = entering(r)
            kept[r, top, :] = moved(other, 0, state, r)
            sent[r, top, :] = state.astype(BF16)
            kept[r, bottom, :] = back.astype(BF16)
            sent[r, bottom, :] = moved(mine, 1, back, r)


def unpair(info, mine, other, parts, after):
    rows, width = parts[0].shape
    count = len(parts)
    return pl.pallas_call(
        following(functools.partial(unpair_kernel, count), 3 + count, len(after)),
        out_shape=[jax.ShapeDtypeStruct((count, 2 * NS, width), BF16)] * 2,
        in_specs=[SMEM] + [VMEM] * (2 + count) + [ANY] * len(after),
        out_specs=[VMEM] * 2,
        cost_estimate=pl.CostEstimate(flops=count * rows * width * 4, bytes_accessed=9 << 20, transcendentals=0),
        name="unpair",
    )(info, mine, other, *parts, *after)


def inner_kernel(
    total_rows, per_group, info, lengths, slow, x, g, w, r, steps, fast, skips,
    out_x, out_w, out_r, cums, flipped, bias,
):
    group = pl.program_id(0)
    rows, heads = steps.shape
    width = per_group * HD

    @pl.when(group == 0)
    def _():
        rates = head_rates(slow, fast[...], total_rows)
        cumulative = running_sums(steps[...], rates)
        cums[...] = cumulative
        flipped[...] = cumulative.T
        base = info[0] * rows
        s = lax.broadcasted_iota(jnp.int32, (rows, rows), 0)
        t = lax.broadcasted_iota(jnp.int32, (rows, rows), 1)
        same = count_before(lengths, base + s) == count_before(lengths, base + t)
        bias[...] = jnp.where(same & (t >= s), 0.0, -jnp.inf)

    one_hot = spread(group, heads, per_group)
    high, low = split(skips[...])
    lowest = (skips[...] - high.astype(F32) - low.astype(F32)).astype(BF16)
    index = lax.broadcasted_iota(jnp.int32, (16, heads), 0)
    table = jnp.where(
        index == 0,
        high.astype(F32),
        jnp.where(index == 1, low.astype(F32), jnp.where(index == 2, lowest.astype(F32), 0.0)),
    ).astype(BF16)
    gains = jnp.sum(dot(table, one_hot), axis=0, keepdims=True)
    ids = lax.broadcasted_iota(jnp.int32, (heads, heads), 1)
    shift = jnp.where(
        lax.broadcasted_iota(jnp.int32, (heads, heads), 0) == ids + group * per_group, 1.0, 0.0
    ).astype(BF16)
    cumulative = cums[...]
    high, low = split(cumulative)
    lowest = (cumulative - high.astype(F32) - low.astype(F32)).astype(BF16)
    columns = dot(high, shift) + dot(low, shift) + dot(lowest, shift)
    across = flipped[pl.ds(pl.multiple_of(group * per_group, per_group), per_group), :]

    write, read = w[...], r[...]
    scores = dot(write, read, NT)
    masked = bias[...]
    left = lax.broadcasted_iota(jnp.int32, (rows, 2 * HD), 1) < HD
    zero = jnp.zeros((rows, 2 * HD), BF16)
    joint = jnp.zeros((rows, rows), F32)
    for m in range(per_group // 2):
        cut = slice(m * 2 * HD, (m + 1) * 2 * HD)
        xs, gs = x[:, cut], g[:, cut]
        pairs = jnp.concatenate([jnp.where(left, xs, zero), jnp.where(left, zero, xs)], axis=0)
        products = dot(pairs, gs, NT)
        mixes = []
        for e in range(2):
            h = 2 * m + e
            gap = across[h : h + 1, :] - columns[:, h : h + 1]
            decay = jnp.exp(gap + masked)
            mixes.append((scores * decay).astype(BF16))
            joint += products[e * rows : (e + 1) * rows, :] * decay
        grads = jnp.concatenate([jnp.where(left, gs, zero), jnp.where(left, zero, gs)], axis=0)
        out_x[:, cut] = (
            dot(jnp.concatenate(mixes, axis=1), grads) + gains[:, cut] * gs.astype(F32)
        )
    joint = joint.astype(BF16)
    out_w[...] = dot(joint, read)
    out_r[...] = dot(joint, write, TN)


def inner(info, lengths, slow, x, g, w, r, steps, fast, skips, total_rows, after):
    rows, heads = steps.shape
    groups = w.shape[1] // NS
    per_group = heads // groups
    width = per_group * HD
    wide = pl.BlockSpec((rows, width), lambda i, *_: (0, i))
    thin = pl.BlockSpec((rows, NS), lambda i, *_: (0, i))
    return pl.pallas_call(
        following(functools.partial(inner_kernel, total_rows, per_group), 10, len(after)),
        out_shape=[
            jax.ShapeDtypeStruct(x.shape, F32),
            jax.ShapeDtypeStruct(w.shape, F32),
            jax.ShapeDtypeStruct(r.shape, F32),
        ],
        grid_spec=pltpu.PrefetchScalarGridSpec(
            num_scalar_prefetch=3,
            grid=(groups,),
            in_specs=[
                wide, wide, thin, thin,
                pl.BlockSpec((rows, heads), lambda i, *_: (0, 0)),
                pl.BlockSpec((1, heads), lambda i, *_: (0, 0)),
                pl.BlockSpec((1, heads), lambda i, *_: (0, 0)),
            ]
            + [ANY] * len(after),
            out_specs=[wide, thin, thin],
            scratch_shapes=[
                pltpu.VMEM((rows, heads), F32),
                pltpu.VMEM((heads, rows), F32),
                pltpu.VMEM((rows, rows), F32),
            ],
        ),
        cost_estimate=pl.CostEstimate(
            flops=rows * rows * heads * 600, bytes_accessed=10 << 20, transcendentals=rows * rows * heads
        ),
        name="inner",
    )(info, lengths, slow, x, g, w, r, steps, fast, skips, *after)


def finish_kernel(
    total_rows, per_group, half, info, lengths, slow, x, g, w, r, steps, fast, part_x, part_w, part_r,
    kept, got, out_x, out_w, out_r, factors, states,
):
    step = pl.program_id(0)
    rows, heads = steps.shape

    @pl.when(step == 0)
    def _():
        rates = head_rates(slow, fast[...], total_rows)
        cumulative = running_sums(steps[...], rates)
        to_end, entering, link = edge_factors(info[0], lengths, cumulative)
        factors[0], factors[1] = split(to_end)
        factors[2], factors[3] = split(entering)

    @pl.when(step < half)
    def _():
        states[...] = kept[0]

    @pl.when(step >= half)
    def _():
        states[...] = got[0]

    owner = jnp.where(step < half, info[2], 1 - info[2])
    group = owner * half + (info[1] ^ (step % half))
    one_hot = spread(group, heads, per_group)
    to_end = dot(factors[0], one_hot) + dot(factors[1], one_hot)
    entering = dot(factors[2], one_hot) + dot(factors[3], one_hot)
    state, back = states[0:NS, :], states[NS : 2 * NS, :]
    out_x[...] = (part_x[...] + to_end * dot(w[...], back)).astype(BF16)
    weighted = (x[...].astype(F32) * to_end).astype(BF16)
    out_w[...] = (part_w[...] + dot(weighted, back, NT)).astype(BF16)
    weighted = (g[...].astype(F32) * entering).astype(BF16)
    out_r[...] = (part_r[...] + dot(weighted, state, NT)).astype(BF16)


def finish(info, lengths, slow, x, g, w, r, steps, fast, parts, kept, got, total_rows):
    rows, heads = steps.shape
    groups = w.shape[1] // NS
    per_group = heads // groups
    width = per_group * HD
    half = groups // 2

    def column(i, info, lengths, slow):
        owner = jnp.where(i < half, info[2], 1 - info[2])
        return (0, owner * half + (info[1] ^ (i % half)))

    wide = pl.BlockSpec((rows, width), column)
    thin = pl.BlockSpec((rows, NS), column)
    return pl.pallas_call(
        functools.partial(finish_kernel, total_rows, per_group, half),
        out_shape=[
            jax.ShapeDtypeStruct(x.shape, BF16),
            jax.ShapeDtypeStruct(w.shape, BF16),
            jax.ShapeDtypeStruct(r.shape, BF16),
        ],
        grid_spec=pltpu.PrefetchScalarGridSpec(
            num_scalar_prefetch=3,
            grid=(groups,),
            in_specs=[
                wide, wide, thin, thin,
                pl.BlockSpec((rows, heads), lambda i, *_: (0, 0)),
                pl.BlockSpec((1, heads), lambda i, *_: (0, 0)),
                wide, thin, thin,
                pl.BlockSpec((1, 2 * NS, width), lambda i, *_: (jnp.minimum(i, half - 1), 0, 0)),
                pl.BlockSpec((1, 2 * NS, width), lambda i, *_: (jnp.maximum(i - half, 0), 0, 0)),
            ],
            out_specs=[wide, thin, thin],
            scratch_shapes=[
                pltpu.VMEM((4, rows, heads), BF16),
                pltpu.VMEM((2 * NS, width), BF16),
            ],
        ),
        cost_estimate=pl.CostEstimate(
            flops=rows * NS * width * groups * 14, bytes_accessed=16 << 20, transcendentals=0
        ),
        name="finish",
    )(info, lengths, slow, x, g, w, r, steps, fast, *parts, kept, got)


def pack_kernel(q, a, k, v, out_qa, out_kv):
    width = out_qa.shape[2] // 2
    for i in range(out_qa.shape[0]):
        out_qa[i, :, 0:width] = q[:, i * width : (i + 1) * width]
        out_qa[i, :, width : 2 * width] = a[:, i * width : (i + 1) * width]
        out_kv[i, :, 0:DH] = k[:, i * DH : (i + 1) * DH]
        out_kv[i, :, DH : 2 * DH] = v[:, i * DH : (i + 1) * DH]


def pack(q, a, k, v):
    rows = q.shape[0]
    count = k.shape[1] // DH
    width = q.shape[1] // count
    tile = rows // 4
    return pl.pallas_call(
        pack_kernel,
        out_shape=[
            jax.ShapeDtypeStruct((count, rows, 2 * width), BF16),
            jax.ShapeDtypeStruct((count, rows, 2 * DH), BF16),
        ],
        grid=(rows // tile,),
        in_specs=[pl.BlockSpec((tile, z.shape[1]), lambda i: (i, 0)) for z in (q, a, k, v)],
        out_specs=[
            pl.BlockSpec((count, tile, 2 * width), lambda i: (0, i, 0)),
            pl.BlockSpec((count, tile, 2 * DH), lambda i: (0, i, 0)),
        ],
        cost_estimate=pl.CostEstimate(flops=0, bytes_accessed=5 << 20, transcendentals=0),
        name="pack",
    )(q, a, k, v)


def unpack_kernel(a, out):
    width = a.shape[2]
    for i in range(a.shape[0]):
        out[:, i * width : (i + 1) * width] = a[i]


def unpack(a):
    count, rows, width = a.shape
    tile = rows // 2
    return pl.pallas_call(
        unpack_kernel,
        out_shape=jax.ShapeDtypeStruct((rows, count * width), BF16),
        grid=(rows // tile,),
        in_specs=[pl.BlockSpec((count, tile, width), lambda i: (0, i, 0))],
        out_specs=pl.BlockSpec((tile, count * width), lambda i: (i, 0)),
        cost_estimate=pl.CostEstimate(flops=0, bytes_accessed=2 << 20, transcendentals=0),
        name="unpack",
    )(a)


def attend_kernel(lead, sizes, rows, info, lengths, qa, *refs):
    parts = refs[: len(sizes)]
    out, keyval, logit, gprob, acc = refs[len(sizes) :]
    block = pl.program_id(0)
    span = qa.shape[0]
    per = qa.shape[1] // (2 * DH)
    scale = DH**-0.5
    first = info[3] * rows

    @pl.when(block == 0)
    def _():
        at = 0
        for part, size in zip(parts, sizes):
            keyval[at : at + size, :] = part[...]
            at += size

    begin = first + block * span
    low = (doc_start(lengths, begin) - (first - lead)) // KEYS
    high = (lead + (block + 1) * span - 1) // KEYS + 1
    position = begin + lax.broadcasted_iota(jnp.int32, (span, DH), 0)
    starts = doc_start(lengths, position)[:, 0:1]
    position = position[:, 0:1]
    query = jnp.concatenate([qa[:, i * DH : (i + 1) * DH] for i in range(per)], axis=0)
    grad = jnp.concatenate([qa[:, (per + i) * DH : (per + i + 1) * DH] for i in range(per)], axis=0)

    def fold(a, op):
        out = a[:, 0:DH]
        for i in range(1, KEYS // DH):
            out = op(out, a[:, i * DH : (i + 1) * DH])
        return out

    def scan(n, peak):
        kv = keyval[pl.ds(pl.multiple_of(n * KEYS, KEYS), KEYS), :]
        raw = dot(query, kv[:, 0:DH], NT)
        where = first - lead + n * KEYS + lax.broadcasted_iota(jnp.int32, (span, KEYS), 1)
        allowed = (where >= starts) & (where <= position)
        raw = jnp.concatenate(
            [jnp.where(allowed, raw[i * span : (i + 1) * span], -jnp.inf) for i in range(per)], axis=0
        )
        logit[n] = raw
        gprob[n] = dot(grad, kv[:, DH : 2 * DH], NT)
        return jnp.maximum(peak, fold(raw, jnp.maximum))

    peak = lax.fori_loop(low, high, scan, jnp.full((per * span, DH), -jnp.inf, F32))
    peak = jnp.max(peak, axis=1, keepdims=True)

    def weigh(n, sums):
        weight = jnp.exp2((logit[n] - peak) * (scale * 1.4426950408889634))
        logit[n] = weight
        return (
            sums[0] + fold(weight, jnp.add),
            sums[1] + fold(weight * gprob[n], jnp.add),
        )

    zero = jnp.zeros((per * span, DH), F32)
    norm, centre = lax.fori_loop(low, high, weigh, (zero, zero))
    norm = jnp.sum(norm, axis=1, keepdims=True)
    centre = jnp.sum(centre, axis=1, keepdims=True) / norm
    inverse = 1.0 / norm
    acc[...] = zero

    def gather(n, carried):
        kv = keyval[pl.ds(pl.multiple_of(n * KEYS, KEYS), KEYS), :]
        pulls = (logit[n] * inverse * (gprob[n] - centre)).astype(BF16)
        acc[...] += dot(pulls, kv[:, 0:DH])
        return carried

    lax.fori_loop(low, high, gather, 0)
    result = acc[...] * scale
    for i in range(per):
        out[:, i * DH : (i + 1) * DH] = result[i * span : (i + 1) * span].astype(BF16)


def attend(info, lengths, qa, parts, lead, rows, after):
    span = 128
    sizes = [part.shape[0] for part in parts]
    keys = sum(sizes)
    width = qa.shape[1]
    per = width // (2 * DH)
    return pl.pallas_call(
        following(functools.partial(attend_kernel, lead, sizes, rows), 3 + len(sizes), len(after)),
        out_shape=jax.ShapeDtypeStruct((qa.shape[0], width // 2), BF16),
        grid_spec=pltpu.PrefetchScalarGridSpec(
            num_scalar_prefetch=2,
            grid=(qa.shape[0] // span,),
            in_specs=[pl.BlockSpec((span, width), lambda i, *_: (i, 0))]
            + [pl.BlockSpec((size, 2 * DH), lambda i, *_: (0, 0)) for size in sizes]
            + [ANY] * len(after),
            out_specs=pl.BlockSpec((span, width // 2), lambda i, *_: (i, 0)),
            scratch_shapes=[
                pltpu.VMEM((keys, 2 * DH), BF16),
                pltpu.VMEM((keys // KEYS, per * span, KEYS), F32),
                pltpu.VMEM((keys // KEYS, per * span, KEYS), F32),
                pltpu.VMEM((per * span, DH), F32),
            ],
        ),
        cost_estimate=pl.CostEstimate(
            flops=qa.shape[0] * per * lead * 6 * DH,
            bytes_accessed=8 << 20,
            transcendentals=qa.shape[0] * per * lead,
        ),
        name="attend",
    )(info, lengths, qa, *parts, *after)


def shards(
    x, w, r, steps, fast_rates, slow_heads, skip_gains, g, queries, keys, values, attn_grad, doc_lengths
):
    ctx_count, head_count = lax.axis_size("ctx"), lax.axis_size("head")
    devices = ctx_count * head_count
    place = lax.axis_index("ctx") * head_count + lax.axis_index("head")
    rows, heads = steps.shape
    groups = w.shape[1] // NS
    half = groups // 2
    total_rows = rows * devices
    lead = REACH * rows * head_count
    plane = rows * groups
    shifts = (lead - 1) // plane + 1
    member = place % groups
    chip, core = member // 2, member % 2
    fast = fast_rates.reshape(1, heads)
    skips = skip_gains.reshape(1, heads)

    def info(*scalars):
        return jnp.stack([jnp.asarray(s, jnp.int32) for s in scalars])

    def swap(value, flip):
        return lax.ppermute(value, AXES, [(i, i ^ flip) for i in range(devices)])

    def shifted(value, steps):
        return lax.ppermute(
            value,
            AXES,
            [(i, i + steps) for i in range(max(0, -steps), min(devices, devices - steps))],
        )

    members = [list(range(i, i + groups)) for i in range(0, devices, groups)]

    def exchange(value):
        return lax.all_to_all(value, AXES, 0, 0, tiled=True, axis_index_groups=members)

    scalars = info(place, chip, core, place - member)

    def half_edges(which):
        return edges(
            info(place, which, chip), doc_lengths, slow_heads, x, g, w, r, steps, fast, total_rows
        )

    sent = half_edges(1 - core)
    other = swap(sent, 1)
    packed_qa, packed_kv = pack(queries, attn_grad, keys, values)
    kv = exchange(packed_kv).reshape(plane, 2 * DH)
    mine = half_edges(core)
    own = pair(scalars, mine, other)
    parts = [own[0]] + [swap(own[i], 2 * i) for i in range(1, half)]

    kv_parts = []
    for k in range(shifts, 0, -1):
        size = min(plane, lead - (k - 1) * plane)
        kv_parts.append(shifted(kv[plane - size :], groups * k))
    kv_parts.append(kv)

    inners = inner(
        scalars, doc_lengths, slow_heads, x, g, w, r, steps, fast, skips, total_rows, [own[0]]
    )
    forward, backward = totals(scalars, parts, [inners[1]])
    behind = [shifted(forward, groups * k) for k in range(1, shifts + 1)]
    ahead = [shifted(backward, -groups * k) for k in range(1, shifts + 1)]
    packed_qa, forward = lax.optimization_barrier((packed_qa, forward))
    qa = exchange(packed_qa).reshape(plane, -1)
    carried = carry(scalars, parts, behind, ahead)
    entered = [carried[0]] + [swap(carried[i], 2 * i) for i in range(1, half)]
    grads = attend(scalars, doc_lengths, qa, kv_parts, lead, rows, [carried[0]])
    back = exchange(grads.reshape(groups, rows, -1))
    kept, to_other = unpair(scalars, mine, other, entered, [grads])
    got = swap(to_other, 1)
    grad_x, grad_w, grad_r = finish(
        scalars, doc_lengths, slow_heads, x, g, w, r, steps, fast, inners, kept, got, total_rows
    )
    return grad_x, grad_w, grad_r, unpack(back)


def solution(mesh):
    rows = P(("ctx", "head"), None)
    return jax.shard_map(
        shards,
        mesh=mesh,
        in_specs=(rows, rows, rows, rows, P(), P(), P(), rows, rows, rows, rows, rows, P()),
        out_specs=(rows, rows, rows, rows),
        check_vma=False,
    )
```
